128 devices in a mesh: tm: 8 (over x, core), tile: 16 (over y, z).
Axes of the slice: x: 4, y: 4, z: 4, core: 2. Of those that a mesh axis runs over, the one named last changes fastest.
Arguments:
- movie_frames: bfloat16 [1024, 32, 4096], P(('tm', 'tile')), may hold values from -6 to 6
- baseline: float32 [32, 4096], replicated, may hold values from -3 to 3
- footprints: bfloat16 [64, 32, 4096], P(None, 'tile'), as said below
- traces: float32 [640, 1024], P('tile', 'tm'), may hold values from 0 to 1
- intersection: int32 [32, 64], P('tile'), may hold values from 0 to 639, as said below
- counts: int32 [32], P('tile'), may hold values from 20 to 64
- offsets: int32 [8, 2], replicated, may hold values from -12 to 12, as said below
- cycle_coef: float32 [8], replicated, may hold values from 0.05 to 0.2
- decay_rate: float32 [640], P('tile'), may hold values from 0.9 to 0.9985
- rise_rate: float32 [640], P('tile'), may hold values from 0.1 to 0.6
- penalty: float32 [640], P('tile'), may hold values from 0.05 to 0.3
Outputs:
- neuron_traces: float32 [640, 1024], P('tile', 'tm')
- neuron_shapes: bfloat16 [64, 32, 4096], P(None, 'tile')
- backdrop: bfloat16 [1024, 32, 4096], P(('tm', 'tile'))
The draws below stay inside these ranges and needn't reach their ends.
Inputs may be any that keep to these rules, and one draw needn't show every extreme that they name: `intersection`: slot s < 20 of tile t names neuron (t // 2) * 40 + s * 2 + t % 2; other slots may name any neuron, repeats allowed. |offsets[r, 0]| + |offsets[r, 1]| = 12 for every r. `footprints`: every entry is positive.
All inputs are finite; a program needn't handle non-finite values.
Results may differ from the reference program's by a relative error of at most 0.0034.
Values may be sent and summed in bfloat16 or wider, within the bound.
No kernel may reach another device: no remote copies, remote signals or barrier semaphores. Data moves between devices by JAX's collectives and lax.ppermute only.
A program may use at most 128 MiB of HBM per device.

```python
import math
import jax
import jax.numpy as jnp
from jax import lax

TSIDE = 64
PIX = 4096
GRID_W = 8
TILE_DEV = 2
TILES = 32
FRAMES = 1024
NEUR_TILE = 20
NEUR_DEV = 40
NEURONS = 640
SLOTS = 64
CYCLE = 8
RAD = 12
ITERS = 2


def draw_footprints(key, part):
    subkeys = jax.random.split(key, 4)
    centre_row = jax.random.uniform(subkeys[0], (SLOTS, TILES, 1), jnp.float32, 0.0, float(TSIDE))
    centre_col = jax.random.uniform(subkeys[1], (SLOTS, TILES, 1), jnp.float32, 0.0, float(TSIDE))
    blob_width = TSIDE / 8.0
    amplitude = jax.random.uniform(subkeys[2], (SLOTS, TILES, 1), jnp.float32, 0.5, 1.5)
    texture = jax.random.uniform(subkeys[3], (SLOTS, TILES, PIX), jnp.float32, 0.6, 1.4)
    position = jnp.arange(PIX, dtype=jnp.int32)
    row_pos = (position // TSIDE).astype(jnp.float32) + 0.5
    col_pos = (position % TSIDE).astype(jnp.float32) + 0.5
    distance = (row_pos - centre_row) * (row_pos - centre_row) + (col_pos - centre_col) * (col_pos - centre_col)
    values = amplitude * texture * (jnp.exp(-distance / (2.0 * blob_width * blob_width)) + 0.05)
    return values.astype(jnp.bfloat16)


def draw_intersection(key, part):
    tile_index = jnp.arange(TILES, dtype=jnp.int32)[:, None]
    slot_index = jnp.arange(SLOTS, dtype=jnp.int32)[None, :]
    home = tile_index // TILE_DEV * NEUR_DEV + slot_index * TILE_DEV + tile_index % TILE_DEV
    extra = jax.random.randint(key, (TILES, SLOTS), 0, NEURONS, dtype=jnp.int32)
    return jnp.where(slot_index < NEUR_TILE, home, extra).astype(jnp.int32)


def draw_counts(key, part):
    subkeys = jax.random.split(key, 3)
    filled = jax.random.randint(subkeys[0], (TILES,), NEUR_TILE, SLOTS + 1, dtype=jnp.int32)
    busiest = jax.random.randint(subkeys[1], (), 0, TILES, dtype=jnp.int32)
    lightest = (busiest + 1 + jax.random.randint(subkeys[2], (), 0, TILES - 1, dtype=jnp.int32)) % TILES
    position = jnp.arange(TILES, dtype=jnp.int32)
    filled = jnp.where(position == busiest, SLOTS, filled)
    filled = jnp.where(position == lightest, NEUR_TILE, filled)
    return filled.astype(jnp.int32)


def draw_offsets(key, part):
    subkeys = jax.random.split(key, 2)
    rows_shift = jax.random.randint(subkeys[0], (CYCLE,), -RAD, RAD + 1, dtype=jnp.int32)
    signs = jax.random.randint(subkeys[1], (CYCLE,), 0, 2, dtype=jnp.int32) * 2 - 1
    cols_shift = signs * (RAD - jnp.abs(rows_shift))
    position = jnp.arange(CYCLE, dtype=jnp.int32)
    axis_rows = jnp.where(position == 0, RAD, jnp.where(position == 1, -RAD, 0))
    axis_cols = jnp.where(position == 2, RAD, jnp.where(position == 3, -RAD, 0))
    rows_shift = jnp.where(position < 4, axis_rows, rows_shift)
    cols_shift = jnp.where(position < 4, axis_cols, cols_shift)
    return jnp.stack([rows_shift, cols_shift], axis=1).astype(jnp.int32)


def draw_decay_rate(key, part):
    lowest = math.log(0.0015)
    highest = math.log(0.1)
    spread = jax.random.uniform(key, (NEURONS,), jnp.float32, lowest, highest)
    return (1.0 - jnp.exp(spread)).astype(jnp.float32)


def block_levels(key, dims, shards, least, largest):
    def one(dim, shards_of):
        heights = jax.random.uniform(jax.random.fold_in(jax.random.fold_in(key, 6), dim), (shards_of,), jnp.float32, least / len(shards), largest / len(shards))
        return jnp.repeat(jnp.exp(heights), dims[dim] // shards_of).reshape((-1,) + (1,) * (len(dims) - dim - 1))

    loudness = one(*shards[0])
    for cut in shards[1:]:
        loudness = loudness * one(*cut)
    return loudness


def scatter_about(own_key, dims, width, most, cuts=(), held_as=jnp.bfloat16):
    array = jax.random.normal(own_key, dims, jnp.float32) * width
    if len(cuts) > 0:
        array = block_levels(own_key, dims, cuts, -0.22, 0.18) * array
    return jnp.clip(array, min=-most, max=most).astype(held_as)


def setup_inputs(seed: int = 0) -> dict:
    arg_keys = jax.random.split(jax.random.key(seed), 12)
    return {
        "movie_frames": scatter_about(arg_keys[0], (FRAMES, TILES, PIX), 1.0, 6.0, ((0, 128),)),
        "baseline": scatter_about(arg_keys[1], (TILES, PIX), 0.5, 3.0, (), jnp.float32),
        "footprints": draw_footprints(jax.random.fold_in(arg_keys[11], 71), 0),
        "traces": jnp.clip(1.0 * jax.random.uniform(arg_keys[3], (NEURONS, FRAMES), jnp.float32) ** block_levels(arg_keys[3], (NEURONS, FRAMES), ((0, 16), (1, 8)), -0.2, 0.2), 0.0, 1.0),
        "intersection": draw_intersection(jax.random.fold_in(arg_keys[11], 71), 0),
        "counts": draw_counts(jax.random.fold_in(arg_keys[11], 71), 0),
        "offsets": draw_offsets(jax.random.fold_in(arg_keys[11], 71), 0),
        "cycle_coef": jnp.clip(jax.random.uniform(arg_keys[7], (CYCLE,), jnp.float32, 0.05, 0.2), 0.05, 0.2),
        "decay_rate": draw_decay_rate(jax.random.fold_in(arg_keys[11], 71), 0),
        "rise_rate": jnp.clip(0.1 + 0.5 * jax.random.uniform(arg_keys[9], (NEURONS,), jnp.float32) ** block_levels(arg_keys[9], (NEURONS,), ((0, 16),), -0.2, 0.2), 0.1, 0.6),
        "penalty": jnp.clip(0.05 + 0.25 * jax.random.uniform(arg_keys[10], (NEURONS,), jnp.float32) ** block_levels(arg_keys[10], (NEURONS,), ((0, 16),), -0.2, 0.2), 0.05, 0.3),
    }


EPSILON = 1e-6
PRECISE = lax.Precision.HIGHEST


def cycle_background(leftover, offsets, cycle_coef):
    frame_count, tiles, pixels = leftover.shape
    tile_rows = tiles // GRID_W
    picture = leftover.reshape(frame_count, tile_rows, GRID_W, TSIDE, TSIDE)
    picture = picture.transpose(0, 1, 3, 2, 4).reshape(frame_count, tile_rows * TSIDE, GRID_W * TSIDE)
    padded = jnp.pad(picture, ((0, 0), (RAD, RAD), (RAD, RAD)))
    summed = jnp.zeros(picture.shape, jnp.float32)
    anchor = jnp.zeros((), jnp.int32)
    for cycle_index in range(offsets.shape[0]):
        row_start = (offsets[cycle_index, 0] + RAD).astype(jnp.int32)
        col_start = (offsets[cycle_index, 1] + RAD).astype(jnp.int32)
        shifted = lax.dynamic_slice(padded, (anchor, row_start, col_start), picture.shape)
        summed = summed + cycle_coef[cycle_index] * shifted.astype(jnp.float32)
    summed = summed.reshape(frame_count, tile_rows, TSIDE, GRID_W, TSIDE).transpose(0, 1, 3, 2, 4)
    return summed.reshape(frame_count, tiles, pixels)


def calcium_filter(rectified, decay_rate, rise_rate):
    coef_one = decay_rate + rise_rate
    coef_two = -decay_rate * rise_rate
    unit_gain = (1.0 - decay_rate) * (1.0 - rise_rate)

    def advance(carry, column):
        previous, older = carry
        present = coef_one * previous + coef_two * older + unit_gain * column
        return (present, previous), present

    zeros = jnp.zeros_like(decay_rate)
    _, filtered = lax.scan(advance, (zeros, zeros), rectified.T)
    return filtered.T


def reference(movie_frames, baseline, footprints, traces, intersection, counts, offsets, cycle_coef, decay_rate, rise_rate, penalty):
    occupied = jnp.arange(SLOTS, dtype=jnp.int32)[None, :] < counts[:, None]
    picker = ((intersection[:, :, None] == jnp.arange(NEURONS, dtype=jnp.int32)[None, None, :]) & occupied[:, :, None]).astype(jnp.float32)
    occupied_rows = occupied.T.astype(jnp.float32)[:, :, None]
    footprint = footprints * occupied_rows.astype(jnp.bfloat16)

    def collect(series):
        rounded = lax.optimization_barrier(series.astype(jnp.bfloat16)).astype(jnp.float32)
        return jnp.einsum("tsk,kf->tsf", picker, rounded, precision=PRECISE).astype(jnp.bfloat16)

    def rebuild(slot_rows, shapes):
        return jnp.einsum("tsf,stp->ftp", slot_rows.astype(jnp.float32), shapes.astype(jnp.float32), precision=PRECISE)

    slot_rows = collect(traces)
    backdrop = jnp.zeros(movie_frames.shape, jnp.bfloat16)
    for iteration in range(ITERS):
        rebuilt = rebuild(slot_rows, footprint)
        leftover = (movie_frames.astype(jnp.float32) - baseline[None] - rebuilt).astype(jnp.bfloat16)
        backdrop = cycle_background(leftover, offsets, cycle_coef).astype(jnp.bfloat16)
        clean = movie_frames.astype(jnp.float32) - baseline[None] - backdrop.astype(jnp.float32)
        misfit = (clean - rebuilt).astype(jnp.bfloat16).astype(jnp.float32)
        shapes_float = footprint.astype(jnp.float32)
        spread = jnp.sum(shapes_float, axis=0)
        projection = jnp.einsum("stp,ftp->tsf", shapes_float, misfit, precision=PRECISE)
        majorizer = jnp.einsum("stp,tp->ts", shapes_float, spread, precision=PRECISE)
        gradient = jnp.einsum("tsk,tsf->kf", picker, projection, precision=PRECISE)
        curvature = jnp.einsum("tsk,ts->k", picker, majorizer, precision=PRECISE)
        stepped = traces + gradient / (curvature + EPSILON)[:, None]
        rectified = jnp.maximum(stepped - penalty[:, None], 0.0)
        traces = calcium_filter(rectified, decay_rate, rise_rate)
        slot_rows = collect(traces)
        rebuilt = rebuild(slot_rows, footprint)
        misfit = (clean - rebuilt).astype(jnp.bfloat16).astype(jnp.float32)
        slot_float = slot_rows.astype(jnp.float32)
        numerator = jnp.einsum("tsf,ftp->stp", slot_float, misfit, precision=PRECISE)
        cluster = jnp.sum(slot_float, axis=1)
        weight = jnp.einsum("tsf,tf->ts", slot_float, cluster, precision=PRECISE)
        divisor = jnp.maximum(weight.T, jnp.float32(1.0))
        footprint = (jnp.maximum(shapes_float + numerator / divisor[:, :, None], 0.0) * occupied_rows).astype(jnp.bfloat16)
    return traces, footprint, backdrop
```

```python
import functools

import jax
import jax.numpy as jnp
from jax import lax
from jax.experimental import pallas as pl
from jax.experimental.pallas import tpu as pltpu
from jax.sharding import PartitionSpec as P

SIDE = 64
WIDE = 128
RAD = 12
STRIP = 16
GRID_W = 8
ITERS = 2
SLOTS = 64
CYCLE = 8
NEUR = 40
NPAD = 48
EPSILON = 1e-06
F32 = jnp.float32
BF16 = jnp.bfloat16


def nt(a, b):
    return lax.dot_general(a, b, (((1,), (1,)), ((), ())), preferred_element_type=F32)


def nn(a, b):
    return lax.dot_general(a, b, (((1,), (0,)), ((), ())), preferred_element_type=F32)


def eye(n):
    return (
        lax.broadcasted_iota(jnp.int32, (n, n), 0) == lax.broadcasted_iota(jnp.int32, (n, n), 1)
    ).astype(BF16)


def three(x):
    high = x.astype(BF16)
    rest = x - high.astype(F32)
    mid = rest.astype(BF16)
    low = (rest - mid.astype(F32)).astype(BF16)
    return high, mid, low


def lane(shape):
    return lax.broadcasted_iota(jnp.int32, shape, len(shape) - 1)


def row(shape):
    return lax.broadcasted_iota(jnp.int32, shape, len(shape) - 2)


def call(body, outs, args, smem=0, scratch=(), name=None):
    spaces = [pl.BlockSpec(memory_space=pltpu.SMEM)] * smem
    spaces += [pl.BlockSpec(memory_space=pltpu.VMEM)] * (len(args) - smem)
    return pl.pallas_call(
        body,
        out_shape=[jax.ShapeDtypeStruct(s, d) for s, d in outs],
        in_specs=spaces,
        out_specs=[pl.BlockSpec(memory_space=pltpu.VMEM)] * len(outs),
        scratch_shapes=list(scratch),
        name=name,
    )(*args)


def doubled(block):
    wide = block.astype(F32)
    first = (lane(wide.shape) & (WIDE - 1)) < SIDE
    upper = jnp.where(first, wide, 0.0)
    return jnp.concatenate([upper, wide - upper], axis=0).astype(BF16)


def baseline_body(base_ref, out_ref):
    unit = eye(256)

    def step(j, carry):
        for t in range(2):
            line = base_ref[t, 0:1, pl.ds(pl.multiple_of(j * 256, 256), 256)]
            parts = three(jnp.broadcast_to(line, (WIDE, 256)))
            col = nt(unit, parts[0]) + nt(unit, parts[1]) + nt(unit, parts[2])
            out_ref[pl.ds(j * 4, 4), t * SIDE : (t + 1) * SIDE, :] = col.reshape(4, SIDE, WIDE)
        return carry

    lax.fori_loop(0, 16, step, 0)


def merge_body(count_ref, fp_ref, out_ref):
    first = lane((SLOTS, WIDE)) < SIDE
    slot = row((SLOTS, WIDE))
    live = slot < jnp.where(first, count_ref[0], count_ref[1])
    for j in range(32):
        a = fp_ref[0, :, j * WIDE : (j + 1) * WIDE].astype(F32)
        b = fp_ref[1, :, j * WIDE : (j + 1) * WIDE].astype(F32)
        even = jnp.where(first, a, pltpu.roll(b, SIDE, 1))
        odd = jnp.where(first, pltpu.roll(a, SIDE, 1), b)
        at = (2 * j) % 8 * WIDE
        out_ref[j // 4, :, at : at + WIDE] = jnp.where(live, even, 0.0).astype(BF16)
        out_ref[j // 4, :, at + WIDE : at + 2 * WIDE] = jnp.where(live, odd, 0.0).astype(BF16)


def split_body(fb_ref, out_ref):
    first = lane((SLOTS, WIDE)) < SIDE
    for j in range(32):
        at = (2 * j) % 8 * WIDE
        even = fb_ref[j // 4, :, at : at + WIDE].astype(F32)
        odd = fb_ref[j // 4, :, at + WIDE : at + 2 * WIDE].astype(F32)
        a = jnp.where(first, even, pltpu.roll(odd, SIDE, 1))
        b = jnp.where(first, pltpu.roll(even, SIDE, 1), odd)
        out_ref[0, :, j * WIDE : (j + 1) * WIDE] = a.astype(BF16)
        out_ref[1, :, j * WIDE : (j + 1) * WIDE] = b.astype(BF16)


def expand_body(fb_ref, out_ref):
    unit = eye(256)

    def step(j, carry):
        both = doubled(fb_ref[j])
        for k in range(4):
            out_ref[j, k * 256 : (k + 1) * 256, :] = nt(
                unit, both[:, k * 256 : (k + 1) * 256]
            ).astype(BF16)
        return carry

    lax.fori_loop(0, 8, step, 0)


def major_body(fb_ref, out_ref):
    def step(j, total):
        for k in range(8):
            block = fb_ref[j, :, k * WIDE : (k + 1) * WIDE].astype(F32)
            total = total + block * jnp.sum(block, axis=0, keepdims=True)
        return total

    total = lax.fori_loop(0, 8, step, jnp.zeros((SLOTS, WIDE), F32))
    first = lane((SLOTS, WIDE)) < SIDE
    upper = jnp.sum(jnp.where(first, total, 0.0), axis=1, keepdims=True)
    lower = jnp.sum(jnp.where(first, 0.0, total), axis=1, keepdims=True)
    out_ref[...] = jnp.broadcast_to(jnp.concatenate([upper, lower], axis=0), (WIDE, WIDE))


def collect_body(g_ref, pick_ref, out_ref):
    keys = g_ref.shape[0] * g_ref.shape[1]
    chosen = (pick_ref[...] == lane((WIDE, keys))).astype(F32).astype(BF16)
    out_ref[...] = nn(chosen, g_ref[...].reshape(keys, WIDE)).astype(BF16)


def rims(left_ref, rim_refs):
    top, bottom, west, east, nw, ne, sw, se = rim_refs
    top[...] = left_ref[:RAD]
    bottom[...] = left_ref[SIDE - RAD :]
    west[...] = left_ref[:, :STRIP]
    east[...] = left_ref[:, WIDE - STRIP :]
    nw[...] = left_ref[:RAD, :STRIP]
    ne[...] = left_ref[:RAD, WIDE - STRIP :]
    sw[...] = left_ref[SIDE - RAD :, :STRIP]
    se[...] = left_ref[SIDE - RAD :, WIDE - STRIP :]


def first_left_body(x_ref, base_ref, ft_ref, s_ref, d_ref, resid_ref, left_ref, *rim_refs):
    unit = eye(256)
    slots = s_ref[...]

    def step(j, carry):
        halves = []
        for t in range(2):
            part = x_ref[:, t, :, pl.ds(pl.multiple_of(j * 256, 256), 256)].astype(F32)
            part = part.reshape(WIDE, 256).astype(BF16)
            halves.append(nt(unit, part).reshape(4, SIDE, WIDE))
        rows = pl.ds(j * 4, 4)
        clean = jnp.concatenate(halves, axis=1) - base_ref[rows]
        ft = ft_ref[j // 2, pl.ds(pl.multiple_of((j % 2) * 512, 512), 512), :]
        resid = clean - nn(ft, slots).reshape(4, WIDE, WIDE)
        d_ref[rows] = clean
        resid_ref[rows] = resid
        left_ref[rows] = resid.astype(BF16)
        return carry

    lax.fori_loop(0, 16, step, 0)
    rims(left_ref, rim_refs)


def next_left_body(fb_ref, d_ref, s_ref, ft_ref, resid_ref, left_ref, *rim_refs):
    unit = eye(256)
    slots = s_ref[...]

    def step(j, carry):
        both = doubled(fb_ref[j])
        for k in range(4):
            ft = nt(unit, both[:, k * 256 : (k + 1) * 256]).astype(BF16)
            ft_ref[j, k * 256 : (k + 1) * 256, :] = ft
            rows = pl.ds(j * 8 + k * 2, 2)
            resid = d_ref[rows] - nn(ft, slots).reshape(2, WIDE, WIDE)
            resid_ref[rows] = resid
            left_ref[rows] = resid.astype(BF16)
        return carry

    lax.fori_loop(0, 8, step, 0)
    rims(left_ref, rim_refs)


def stencil_body(
    off_ref, coef_ref, left_ref, top, bottom, west, east, nw, ne, sw, se,
    resid_ref, fb_ref, major_ref, pick_ref, drop_ref, out_ref, pad_ref, mis_ref,
):
    first, last = RAD, RAD + SIDE
    inner, outer = STRIP, STRIP + WIDE

    def fill(r, carry):
        pad_ref[first + r, inner:outer, :] = left_ref[r].astype(F32)
        pad_ref[first + r, :inner, :] = west[r].astype(F32)
        pad_ref[first + r, outer:, :] = east[r].astype(F32)
        return carry

    lax.fori_loop(0, SIDE, fill, 0)

    def ends(r, carry):
        pad_ref[r, inner:outer, :] = top[r].astype(F32)
        pad_ref[r, :inner, :] = nw[r].astype(F32)
        pad_ref[r, outer:, :] = ne[r].astype(F32)
        pad_ref[last + r, inner:outer, :] = bottom[r].astype(F32)
        pad_ref[last + r, :inner, :] = sw[r].astype(F32)
        pad_ref[last + r, outer:, :] = se[r].astype(F32)
        return carry

    lax.fori_loop(0, RAD, ends, 0)

    def step(r, carry):
        total = jnp.zeros((WIDE, WIDE), F32)
        for i in range(CYCLE):
            source = pad_ref[r + RAD + off_ref[i, 0], pl.ds(STRIP + off_ref[i, 1], WIDE), :]
            total = total + coef_ref[i] * source
        drop = total.astype(BF16)
        drop_ref[r] = drop
        mis_ref[r] = (resid_ref[r] - drop.astype(F32)).astype(BF16)
        return carry

    lax.fori_loop(0, SIDE, step, 0)

    total = jnp.zeros((WIDE, WIDE), F32)
    for j in range(8):
        total = total + nn(
            doubled(fb_ref[j]), mis_ref[j * 8 : (j + 1) * 8].reshape(8 * WIDE, WIDE)
        )
    keys = out_ref.shape[0] * NPAD
    chosen = (pick_ref[...] == row((keys, WIDE))).astype(F32).astype(BF16)
    both = jnp.concatenate([total, major_ref[...]], axis=1)
    high, mid, low = three(both)
    found = nn(chosen, high) + nn(chosen, mid) + nn(chosen, low)
    diagonal = row((NPAD, WIDE)) == lane((NPAD, WIDE))
    for b in range(out_ref.shape[0]):
        out_ref[b] = found[b * NPAD : (b + 1) * NPAD, :WIDE]
        spread = jnp.where(diagonal, found[b * NPAD : (b + 1) * NPAD, WIDE:], 0.0)
        out_ref[b, NEUR:NPAD, :] = jnp.broadcast_to(
            jnp.sum(spread, axis=0, keepdims=True), (NPAD - NEUR, WIDE)
        )


def first_order(x, rate):
    at = lane(x.shape)
    power = rate
    for k in range(7):
        x = x + power * jnp.where(at >= (1 << k), pltpu.roll(x, 1 << k, 1), 0.0)
        power = power * power
    return x


def filter_body(sum_ref, traces_ref, decay_ref, rise_ref, penalty_ref, a_ref, b_ref, out_ref):
    total = jnp.sum(sum_ref[...], axis=0)
    gradient = total[:NEUR]
    diagonal = row((NEUR, WIDE)) == lane((NEUR, WIDE))
    spread = jnp.where(diagonal, jnp.broadcast_to(total[NEUR : NEUR + 1], (NEUR, WIDE)), 0.0)
    curvature = jnp.sum(spread, axis=1, keepdims=True)
    decay, rise = decay_ref[...], rise_ref[...]
    stepped = traces_ref[...] + gradient / (curvature + EPSILON)
    rectified = jnp.maximum(stepped - penalty_ref[...], 0.0)
    driven = (1.0 - decay) * (1.0 - rise) * rectified
    a = first_order(driven, decay)
    b = first_order(driven, rise)
    a_ref[...] = a
    b_ref[...] = b
    ends = []
    for x in (a, b):
        at_end = jnp.broadcast_to(x[:, WIDE - 1 :], (NEUR, WIDE))
        ends.append(jnp.sum(jnp.where(diagonal, at_end, 0.0), axis=0, keepdims=True))
    ends.append(jnp.zeros((6, WIDE), F32))
    block = jnp.concatenate(ends, axis=0)
    for k in range(out_ref.shape[0]):
        out_ref[k] = block


def entering_body(
    here_ref, ends_ref, rates_ref, a_ref, b_ref, decay_ref, rise_ref, out_ref, copies_ref
):
    here = here_ref[0]
    rates = rates_ref[...]
    for _ in range(7):
        rates = rates * rates
    held = jnp.zeros((8, WIDE), F32)
    for k in range(ends_ref.shape[0]):
        held = jnp.where(k < here, rates * held + ends_ref[k], held)
    diagonal = row((NEUR, WIDE)) == lane((NEUR, WIDE))
    later = lane((NEUR, WIDE)) + 1

    def whole(x, rate, line):
        spread = jnp.where(diagonal, jnp.broadcast_to(line, (NEUR, WIDE)), 0.0)
        entering = jnp.sum(spread, axis=1, keepdims=True)
        powers = jnp.ones((NEUR, WIDE), F32)
        squared = rate
        for k in range(8):
            powers = powers * jnp.where((later >> k) & 1 == 1, squared, 1.0)
            squared = squared * squared
        return x + powers * entering

    decay, rise = decay_ref[...], rise_ref[...]
    a = whole(a_ref[...], decay, held[0:1])
    b = whole(b_ref[...], rise, held[1:2])
    traces = (decay * a - rise * b) / (decay - rise)
    out_ref[...] = traces
    padded = jnp.concatenate([traces, jnp.zeros((NPAD - NEUR, WIDE), F32)], axis=0).astype(BF16)
    for k in range(copies_ref.shape[0]):
        copies_ref[k] = padded


def numer_body(g_ref, pick_ref, d_ref, drop_ref, ft_ref, s_ref, out_ref):
    keys = g_ref.shape[0] * g_ref.shape[1]
    chosen = (pick_ref[...] == lane((WIDE, keys))).astype(F32).astype(BF16)
    slots = nn(chosen, g_ref[...].reshape(keys, WIDE)).astype(BF16)
    s_ref[...] = slots
    wide = slots.astype(F32)
    sums = jnp.concatenate(
        [
            jnp.broadcast_to(jnp.sum(wide[:SLOTS], axis=0, keepdims=True), (SLOTS, WIDE)),
            jnp.broadcast_to(jnp.sum(wide[SLOTS:], axis=0, keepdims=True), (SLOTS, WIDE)),
        ],
        axis=0,
    )
    weight = jnp.sum(wide * sums, axis=1, keepdims=True)
    first = lane((SLOTS, WIDE)) < SIDE
    weights = jnp.where(first, weight[:SLOTS], weight[SLOTS:])
    first = (lane((SLOTS, 8 * WIDE)) & (WIDE - 1)) < SIDE

    def step(j, carry):
        rebuilt = nn(ft_ref[j], slots)
        rows = pl.ds(j * 8, 8)
        clean = d_ref[rows] - drop_ref[rows].astype(F32)
        mis = (clean.reshape(8 * WIDE, WIDE) - rebuilt).astype(BF16)
        both = nt(slots, mis)
        out_ref[j, :, : 8 * WIDE] = jnp.where(first, both[:SLOTS], both[SLOTS:])
        out_ref[j, :, 8 * WIDE :] = weights
        return carry

    lax.fori_loop(0, 8, step, 0)


def update_body(info_ref, parts_ref, fb_ref, out_ref):
    first = lane((SLOTS, WIDE)) < SIDE
    slot = row((SLOTS, WIDE))
    live = slot < jnp.where(first, info_ref[1], info_ref[2])
    here = info_ref[0]
    count = parts_ref.shape[0]

    def total(at):
        part = parts_ref[0, :, at : at + WIDE]
        for k in range(1, count):
            part = part + parts_ref[k, :, at : at + WIDE]
        return part

    divisor = jnp.maximum(total(8 * WIDE), 1.0)
    for j in range(8):
        at = j * WIDE
        current = fb_ref[here, :, at : at + WIDE].astype(F32)
        fresh = jnp.maximum(current + total(at) / divisor, 0.0)
        fresh = jnp.where(live, fresh, 0.0).astype(BF16)
        for k in range(out_ref.shape[0]):
            out_ref[k, :, at : at + WIDE] = fresh


def frames_body(drop_ref, out_ref):
    unit = eye(WIDE)

    def step(j, carry):
        for t in range(2):
            part = drop_ref[pl.ds(j * 4, 4), t * SIDE : (t + 1) * SIDE, :].reshape(256, WIDE)
            turned = nt(unit, part).reshape(16, 8, 256)
            out_ref[:, t, :, pl.ds(pl.multiple_of(j * 256, 256), 256)] = turned.astype(BF16)
        return carry

    lax.fori_loop(0, 16, step, 0)


def swapped(x, axis):
    return lax.all_to_all(x, axis, split_axis=0, concat_axis=0, tiled=True)


def rim_exchange(rims_here, across):
    top, bottom, west, east, nw, ne, sw, se = rims_here
    count = lax.axis_size("tile")

    def moved(piece, down, right):
        pairs = []
        for source in range(count):
            y, x = source // across + down, source % across + right
            if 0 <= y < count // across and 0 <= x < across:
                pairs.append((source, y * across + x))
        return lax.ppermute(piece, "tile", pairs)

    return (
        moved(bottom, 1, 0),
        moved(top, -1, 0),
        moved(east, 0, 1),
        moved(west, 0, -1),
        moved(se, 1, 1),
        moved(sw, 1, -1),
        moved(ne, -1, 1),
        moved(nw, -1, -1),
    )


def body(
    movie_frames,
    baseline,
    footprints,
    traces,
    intersection,
    counts,
    offsets,
    cycle_coef,
    decay_rate,
    rise_rate,
    penalty,
):
    tiles, frames = lax.axis_size("tile"), lax.axis_size("tm")
    frames_dev = movie_frames.shape[0]
    pixels = SIDE * SIDE
    here = lax.axis_index("tile")
    block = lax.axis_index("tm").astype(jnp.int32)
    picture = (SIDE, WIDE, WIDE)

    ready = movie_frames.reshape(frames_dev, tiles, 2, pixels).transpose(1, 2, 0, 3)
    local_movie = swapped(ready, "tile")

    base = lax.dynamic_slice_in_dim(baseline, here * 2, 2, 0).reshape(2, 1, pixels)
    occupied = jnp.arange(SLOTS, dtype=jnp.int32)[None, :] < counts[:, None]
    owner = intersection // NEUR
    pick = jnp.where(occupied, owner * NPAD + (intersection - owner * NEUR), -1).reshape(-1)
    pick_row, pick_col = pick.reshape(1, WIDE), pick.reshape(WIDE, 1)
    decay, rise, cost = (v.reshape(NEUR, 1) for v in (decay_rate, rise_rate, penalty))
    rates = jnp.zeros((8, WIDE), F32).at[0, :NEUR].set(decay_rate).at[1, :NEUR].set(rise_rate)
    info = jnp.concatenate([block.reshape(1), counts])

    padded = jnp.pad(traces, ((0, NPAD - NEUR), (0, 0))).astype(BF16)
    gathered = swapped(jnp.broadcast_to(padded, (tiles, NPAD, WIDE)), "tile")
    (base_cols,) = call(baseline_body, [(picture, F32)], (base,), name="base")
    (shapes,) = call(
        merge_body,
        [((8, SLOTS, 8 * WIDE), BF16)],
        (counts, footprints.transpose(1, 0, 2)),
        smem=1,
        name="merge",
    )
    (turned,) = call(expand_body, [((8, 8 * WIDE, WIDE), BF16)], (shapes,), name="expand")
    (slots,) = call(
        collect_body, [((WIDE, WIDE), BF16)], (gathered, pick_col), name="collect"
    )
    rim_shapes = [
        ((RAD, WIDE, WIDE), BF16),
        ((RAD, WIDE, WIDE), BF16),
        ((SIDE, STRIP, WIDE), BF16),
        ((SIDE, STRIP, WIDE), BF16),
    ] + [((RAD, STRIP, WIDE), BF16)] * 4
    drop = None
    clean = None
    for iteration in range(ITERS):
        (major,) = call(major_body, [((WIDE, WIDE), F32)], (shapes,), name="major")
        if iteration == 0:
            clean, resid, left, *rim = call(
                first_left_body,
                [(picture, F32), (picture, F32), (picture, BF16)] + rim_shapes,
                (local_movie, base_cols, turned, slots),
                name="left0",
            )
        else:
            turned, resid, left, *rim = call(
                next_left_body,
                [((8, 8 * WIDE, WIDE), BF16), (picture, F32), (picture, BF16)] + rim_shapes,
                (shapes, clean, slots),
                name="left1",
            )
        around = rim_exchange(rim, GRID_W // 2)
        up, down, left_side, right_side, nw, ne, sw, se = around
        drop, terms = call(
            stencil_body,
            [(picture, BF16), ((tiles, NPAD, WIDE), F32)],
            (offsets, cycle_coef, left, up, down, left_side, right_side, nw, ne, sw, se,
             resid, shapes, major, pick_row),
            smem=2,
            scratch=[
                pltpu.VMEM((SIDE + 2 * RAD, WIDE + 2 * STRIP, WIDE), F32),
                pltpu.VMEM(picture, BF16),
            ],
            name="stencil",
        )
        arrived = swapped(terms, "tile")
        a, b, ends = call(
            filter_body,
            [((NEUR, WIDE), F32), ((NEUR, WIDE), F32), ((frames, 8, WIDE), F32)],
            (arrived, traces, decay, rise, cost),
            name="filter",
        )
        ends = swapped(ends, "tm")
        traces, copies = call(
            entering_body,
            [((NEUR, WIDE), F32), ((tiles, NPAD, WIDE), BF16)],
            (block.reshape(1), ends, rates, a, b, decay, rise),
            smem=1,
            name="entering",
        )
        gathered = swapped(copies, "tile")
        slots, numer = call(
            numer_body,
            [((WIDE, WIDE), BF16), ((frames, SLOTS, 9 * WIDE), F32)],
            (gathered, pick_col, clean, drop, turned),
            name="numer",
        )
        parts = swapped(numer, "tm")
        (fresh,) = call(
            update_body,
            [((frames, SLOTS, 8 * WIDE), BF16)],
            (info, parts, shapes),
            smem=1,
            name="update",
        )
        shapes = swapped(fresh, "tm")
    (by_frame,) = call(frames_body, [((tiles, 2, frames_dev, pixels), BF16)], (drop,), name="turn")
    backdrop = swapped(by_frame, "tile").transpose(2, 0, 1, 3).reshape(movie_frames.shape)
    (out_shapes,) = call(split_body, [((2, SLOTS, pixels), BF16)], (shapes,), name="split")
    return (traces, out_shapes.transpose(1, 0, 2), backdrop)


def solution(mesh):
    in_specs = (
        P(("tm", "tile"), None, None),
        P(),
        P(None, "tile", None),
        P("tile", "tm"),
        P("tile", None),
        P("tile"),
        P(),
        P(),
        P("tile"),
        P("tile"),
        P("tile"),
    )
    out_specs = (P("tile", "tm"), P(None, "tile", None), P(("tm", "tile"), None, None))
    return jax.shard_map(body, mesh=mesh, in_specs=in_specs, out_specs=out_specs, check_vma=False)
```

```python
import functools

import jax
import jax.numpy as jnp
from jax import lax
from jax.experimental import pallas as pl
from jax.experimental.pallas import tpu as pltpu
from jax.sharding import PartitionSpec as P

SIDE = 64
WIDE = 128
RAD = 12
STRIP = 16
GRID_W = 8
ITERS = 2
SLOTS = 64
CYCLE = 8
NEUR = 40
NPAD = 48
EPSILON = 1e-06
F32 = jnp.float32
BF16 = jnp.bfloat16


def nt(a, b):
    return lax.dot_general(a, b, (((1,), (1,)), ((), ())), preferred_element_type=F32)


def nn(a, b):
    return lax.dot_general(a, b, (((1,), (0,)), ((), ())), preferred_element_type=F32)


def eye(n):
    return (
        lax.broadcasted_iota(jnp.int32, (n, n), 0) == lax.broadcasted_iota(jnp.int32, (n, n), 1)
    ).astype(BF16)


def three(x):
    high = x.astype(BF16)
    rest = x - high.astype(F32)
    mid = rest.astype(BF16)
    low = (rest - mid.astype(F32)).astype(BF16)
    return high, mid, low


def lane(shape):
    return lax.broadcasted_iota(jnp.int32, shape, len(shape) - 1)


def row(shape):
    return lax.broadcasted_iota(jnp.int32, shape, len(shape) - 2)


def call(body, outs, args, smem=0, scratch=(), name=None, room=6, aliases=None):
    spaces = [pl.BlockSpec(memory_space=pltpu.SMEM)] * smem
    spaces += [pl.BlockSpec(memory_space=pltpu.VMEM)] * (len(args) - smem)
    held = [pltpu.with_memory_space_constraint(a, pltpu.VMEM) for a in args[smem:]]
    return pl.pallas_call(
        body,
        out_shape=[pltpu.VMEM(s, d) for s, d in outs],
        in_specs=spaces,
        out_specs=[pl.BlockSpec(memory_space=pltpu.VMEM)] * len(outs),
        scratch_shapes=list(scratch),
        input_output_aliases=aliases or {},
        compiler_params=pltpu.CompilerParams(vmem_limit_bytes=room << 20),
        name=name,
    )(*args[:smem], *held)


def column(line, rows):
    diagonal = row((rows, WIDE)) == lane((rows, WIDE))
    spread = jnp.where(diagonal, jnp.broadcast_to(line, (rows, WIDE)), 0.0)
    return jnp.sum(spread, axis=1, keepdims=True)


def picked(g_ref, pick_ref):
    keys = g_ref.shape[0] * g_ref.shape[1]
    wanted = column(pick_ref[0:1], WIDE).astype(jnp.int32)
    chosen = (wanted == lane((WIDE, keys))).astype(F32).astype(BF16)
    return nn(chosen, g_ref[...].reshape(keys, WIDE)).astype(BF16)


def doubled(block):
    wide = block.astype(F32)
    first = (lane(wide.shape) & (WIDE - 1)) < SIDE
    upper = jnp.where(first, wide, 0.0)
    return jnp.concatenate([upper, wide - upper], axis=0).astype(BF16)


def baseline_body(base_ref, out_ref):
    unit = eye(256)

    def step(j, carry):
        for t in range(2):
            line = base_ref[t, 0:1, pl.ds(pl.multiple_of(j * 256, 256), 256)]
            parts = three(jnp.broadcast_to(line, (WIDE, 256)))
            col = nt(unit, parts[0]) + nt(unit, parts[1]) + nt(unit, parts[2])
            out_ref[pl.ds(j * 4, 4), t * SIDE : (t + 1) * SIDE, :] = col.reshape(4, SIDE, WIDE)
        return carry

    lax.fori_loop(0, 16, step, 0)


def merge_body(info_ref, fp_ref, out_ref):
    first = lane((SLOTS, WIDE)) < SIDE
    slot = row((SLOTS, WIDE))
    live = slot < jnp.where(first, info_ref[1], info_ref[2])
    for j in range(32):
        a = fp_ref[0, :, j * WIDE : (j + 1) * WIDE].astype(F32)
        b = fp_ref[1, :, j * WIDE : (j + 1) * WIDE].astype(F32)
        even = jnp.where(first, a, pltpu.roll(b, SIDE, 1))
        odd = jnp.where(first, pltpu.roll(a, SIDE, 1), b)
        at = (2 * j) % 8 * WIDE
        out_ref[j // 4, :, at : at + WIDE] = jnp.where(live, even, 0.0).astype(BF16)
        out_ref[j // 4, :, at + WIDE : at + 2 * WIDE] = jnp.where(live, odd, 0.0).astype(BF16)


def split_body(info_ref, *refs):
    blocks, out_ref = refs[:-1], refs[-1]
    first = lane((SLOTS, WIDE)) < SIDE
    for block_ref, j in zip(blocks, owners(info_ref)):
        for k in range(4):
            at = 2 * k * WIDE
            even = block_ref[:, at : at + WIDE].astype(F32)
            odd = block_ref[:, at + WIDE : at + 2 * WIDE].astype(F32)
            a = jnp.where(first, even, pltpu.roll(odd, SIDE, 1))
            b = jnp.where(first, pltpu.roll(even, SIDE, 1), odd)
            to = pl.ds(pl.multiple_of((j * 4 + k) * WIDE, WIDE), WIDE)
            out_ref[0, :, to] = a.astype(BF16)
            out_ref[1, :, to] = b.astype(BF16)


def expand_body(fb_ref, out_ref):
    unit = eye(256)

    def step(j, carry):
        both = doubled(fb_ref[j])
        for k in range(4):
            out_ref[j, k * 256 : (k + 1) * 256, :] = nt(
                unit, both[:, k * 256 : (k + 1) * 256]
            ).astype(BF16)
        return carry

    lax.fori_loop(0, 8, step, 0)


def major_body(fb_ref, out_ref):
    def step(j, total):
        for k in range(8):
            block = fb_ref[j, :, k * WIDE : (k + 1) * WIDE].astype(F32)
            total = total + block * jnp.sum(block, axis=0, keepdims=True)
        return total

    total = lax.fori_loop(0, 8, step, jnp.zeros((SLOTS, WIDE), F32))
    first = lane((SLOTS, WIDE)) < SIDE
    upper = jnp.sum(jnp.where(first, total, 0.0), axis=1, keepdims=True)
    lower = jnp.sum(jnp.where(first, 0.0, total), axis=1, keepdims=True)
    out_ref[...] = jnp.broadcast_to(jnp.concatenate([upper, lower], axis=0), (WIDE, WIDE))


def collect_body(g_ref, lines_ref, out_ref):
    out_ref[...] = picked(g_ref, lines_ref)


def sides(left_ref, west, east):
    west[...] = left_ref[:, :STRIP]
    east[...] = left_ref[:, WIDE - STRIP :]


def first_left_body(x_ref, base_ref, ft_ref, s_ref, d_ref, resid_ref, left_ref, west, east):
    unit = eye(256)
    slots = s_ref[...]

    def step(j, carry):
        halves = []
        for t in range(2):
            part = x_ref[:, t, :, pl.ds(pl.multiple_of(j * 256, 256), 256)].astype(F32)
            part = part.reshape(WIDE, 256).astype(BF16)
            halves.append(nt(unit, part).reshape(4, SIDE, WIDE))
        rows = pl.ds(j * 4, 4)
        clean = jnp.concatenate(halves, axis=1) - base_ref[rows]
        ft = ft_ref[j // 2, pl.ds(pl.multiple_of((j % 2) * 512, 512), 512), :]
        resid = clean - nn(ft, slots).reshape(4, WIDE, WIDE)
        d_ref[rows] = clean
        resid_ref[rows] = resid
        left_ref[rows] = resid.astype(BF16)
        return carry

    lax.fori_loop(0, 16, step, 0)
    sides(left_ref, west, east)


def owners(info_ref):
    x, core = info_ref[0] // 2, info_ref[0] % 2
    found = []
    for side in (core, 1 - core):
        for away in (0, -1, 1, 2):
            found.append(lax.rem(x + away + 4, 4) * 2 + side)
    return found


def next_left_body(info_ref, *refs):
    blocks, (d_ref, s_ref, fb_ref, ft_ref, resid_ref, left_ref, west, east) = refs[:8], refs[8:]
    unit = eye(256)
    slots = s_ref[...]
    for block_ref, j in zip(blocks, owners(info_ref)):
        fb_ref[j] = block_ref[...]
        both = doubled(block_ref[...])
        for k in range(4):
            ft = nt(unit, both[:, k * 256 : (k + 1) * 256]).astype(BF16)
            ft_ref[j, k * 256 : (k + 1) * 256, :] = ft
            rows = pl.ds(j * 8 + k * 2, 2)
            resid = d_ref[rows] - nn(ft, slots).reshape(2, WIDE, WIDE)
            resid_ref[rows] = resid
            left_ref[rows] = resid.astype(BF16)
    sides(left_ref, west, east)


def shelf_body(left_ref, west, east, top, bottom):
    for at, out in ((0, top), (SIDE - RAD, bottom)):
        rows = slice(at, at + RAD)
        out[:, :STRIP] = west[rows]
        out[:, STRIP : STRIP + WIDE] = left_ref[rows]
        out[:, STRIP + WIDE :] = east[rows]


def drops(first, last, info_ref, coef_ref, pad_ref, resid_ref, drop_ref, mis_ref):
    def step(r, carry):
        total = jnp.zeros((WIDE, WIDE), F32)
        for i in range(CYCLE):
            down, right = info_ref[3 + 2 * i], info_ref[4 + 2 * i]
            total = total + coef_ref[i] * pad_ref[r + RAD + down, pl.ds(STRIP + right, WIDE), :]
        drop = total.astype(BF16)
        drop_ref[r] = drop
        mis_ref[r] = (resid_ref[r] - drop.astype(F32)).astype(BF16)
        return carry

    lax.fori_loop(first, last, step, 0)


def projected(blocks, fb_ref, mis_ref):
    total = jnp.zeros((WIDE, WIDE), F32)
    for j in blocks:
        total = total + nn(
            doubled(fb_ref[j]), mis_ref[j * 8 : (j + 1) * 8].reshape(8 * WIDE, WIDE)
        )
    return total


def inner_body(
    info_ref, coef_ref, left_ref, west, east, resid_ref, fb_ref, pad_ref, drop_ref, mis_ref, out_ref
):
    def fill(r, carry):
        pad_ref[RAD + r, STRIP : STRIP + WIDE, :] = left_ref[r].astype(F32)
        pad_ref[RAD + r, :STRIP, :] = west[r].astype(F32)
        pad_ref[RAD + r, STRIP + WIDE :, :] = east[r].astype(F32)
        return carry

    lax.fori_loop(0, SIDE, fill, 0)
    drops(RAD, SIDE - RAD, info_ref, coef_ref, pad_ref, resid_ref, drop_ref, mis_ref)
    out_ref[...] = projected(range(2, 6), fb_ref, mis_ref)


def outer_body(
    info_ref, coef_ref, top, bottom, resid_ref, fb_ref, major_ref, lines_ref, part_ref,
    pad_in, drop_in, mis_in, pad_ref, drop_ref, mis_ref, out_ref,
):
    def fill(r, carry):
        pad_ref[r] = top[r].astype(F32)
        pad_ref[RAD + SIDE + r] = bottom[r].astype(F32)
        return carry

    lax.fori_loop(0, RAD, fill, 0)
    drops(0, RAD, info_ref, coef_ref, pad_ref, resid_ref, drop_ref, mis_ref)
    drops(SIDE - RAD, SIDE, info_ref, coef_ref, pad_ref, resid_ref, drop_ref, mis_ref)
    total = part_ref[...] + projected((0, 1, 6, 7), fb_ref, mis_ref)
    keys = out_ref.shape[0] * NPAD
    chosen = (lines_ref[0:1].astype(jnp.int32) == row((keys, WIDE))).astype(F32).astype(BF16)
    both = jnp.concatenate([total, major_ref[...]], axis=1)
    high, mid, low = three(both)
    found = nn(chosen, high) + nn(chosen, mid) + nn(chosen, low)
    diagonal = row((NPAD, WIDE)) == lane((NPAD, WIDE))
    for b in range(out_ref.shape[0]):
        out_ref[b, :NEUR] = found[b * NPAD : b * NPAD + NEUR, :WIDE]
        spread = jnp.where(diagonal, found[b * NPAD : (b + 1) * NPAD, WIDE:], 0.0)
        out_ref[b, NEUR:NPAD, :] = jnp.broadcast_to(
            jnp.sum(spread, axis=0, keepdims=True), (NPAD - NEUR, WIDE)
        )


def first_order(x, rate):
    at = lane(x.shape)
    power = rate
    for k in range(7):
        x = x + power * jnp.where(at >= (1 << k), pltpu.roll(x, 1 << k, 1), 0.0)
        power = power * power
    return x


def filter_body(sum_ref, traces_ref, lines_ref, a_ref, b_ref, out_ref):
    total = jnp.sum(sum_ref[...], axis=0)
    gradient = total[:NEUR]
    diagonal = row((NEUR, WIDE)) == lane((NEUR, WIDE))
    curvature = column(total[NEUR : NEUR + 1], NEUR)
    decay, rise, cost = (column(lines_ref[k : k + 1], NEUR) for k in (1, 2, 3))
    stepped = traces_ref[...] + gradient / (curvature + EPSILON)
    rectified = jnp.maximum(stepped - cost, 0.0)
    driven = (1.0 - decay) * (1.0 - rise) * rectified
    a = first_order(driven, decay)
    b = first_order(driven, rise)
    a_ref[...] = a
    b_ref[...] = b
    ends = []
    for x in (a, b):
        at_end = jnp.broadcast_to(x[:, WIDE - 1 :], (NEUR, WIDE))
        ends.append(jnp.sum(jnp.where(diagonal, at_end, 0.0), axis=0, keepdims=True))
    ends.append(jnp.zeros((6, WIDE), F32))
    block = jnp.concatenate(ends, axis=0)
    for k in range(out_ref.shape[0]):
        out_ref[k] = block


def entering_body(info_ref, ends_ref, lines_ref, a_ref, b_ref, out_ref, copies_ref):
    here = info_ref[0]
    rates = lines_ref[1:3]
    for _ in range(7):
        rates = rates * rates
    held = jnp.zeros((2, WIDE), F32)
    for k in range(ends_ref.shape[0]):
        held = jnp.where(k < here, rates * held + ends_ref[k, :2], held)
    later = lane((NEUR, WIDE)) + 1

    def whole(x, rate, line):
        powers = jnp.ones((NEUR, WIDE), F32)
        squared = rate
        for k in range(8):
            powers = powers * jnp.where((later >> k) & 1 == 1, squared, 1.0)
            squared = squared * squared
        return x + powers * column(line, NEUR)

    decay, rise = (column(lines_ref[k : k + 1], NEUR) for k in (1, 2))
    a = whole(a_ref[...], decay, held[0:1])
    b = whole(b_ref[...], rise, held[1:2])
    traces = (decay * a - rise * b) / (decay - rise)
    out_ref[...] = traces
    padded = jnp.concatenate([traces, jnp.zeros((NPAD - NEUR, WIDE), F32)], axis=0).astype(BF16)
    for k in range(copies_ref.shape[0]):
        copies_ref[k] = padded


def numer_body(info_ref, g_ref, lines_ref, d_ref, drop_ref, ft_ref, s_ref, keep_ref, send_ref):
    slots = picked(g_ref, lines_ref)
    s_ref[...] = slots
    wide = slots.astype(F32)
    sums = jnp.concatenate(
        [
            jnp.broadcast_to(jnp.sum(wide[:SLOTS], axis=0, keepdims=True), (SLOTS, WIDE)),
            jnp.broadcast_to(jnp.sum(wide[SLOTS:], axis=0, keepdims=True), (SLOTS, WIDE)),
        ],
        axis=0,
    )
    weight = jnp.sum(wide * sums, axis=1, keepdims=True)
    first = lane((SLOTS, WIDE)) < SIDE
    weights = jnp.where(first, weight[:SLOTS], weight[SLOTS:])
    first = (lane((SLOTS, 8 * WIDE)) & (WIDE - 1)) < SIDE
    core = info_ref[0] % 2
    for out_ref, side in ((send_ref, 1 - core), (keep_ref, core)):

        def step(x, carry):
            j = 2 * x + side
            rebuilt = nn(ft_ref[j], slots)
            rows = pl.ds(j * 8, 8)
            clean = d_ref[rows] - drop_ref[rows].astype(F32)
            mis = (clean.reshape(8 * WIDE, WIDE) - rebuilt).astype(BF16)
            both = nt(slots, mis)
            out_ref[x, :, : 8 * WIDE] = jnp.where(first, both[:SLOTS], both[SLOTS:])
            out_ref[x, :, 8 * WIDE :] = weights
            return carry

        lax.fori_loop(0, 4, step, 0)


def fold_body(info_ref, keep_ref, got_ref, own_ref, *out_refs):
    x = info_ref[0] // 2
    own_ref[...] = keep_ref[x] + got_ref[x]
    for away, out_ref in zip((1, -1, 2), out_refs):
        there = lax.rem(x + away + 4, 4)
        out_ref[:, : 8 * WIDE] = (
            keep_ref[there, :, : 8 * WIDE] + got_ref[there, :, : 8 * WIDE]
        ).astype(BF16)
        weights = keep_ref[there, :, 8 * WIDE :] + got_ref[there, :, 8 * WIDE :]
        high = weights.astype(BF16)
        out_ref[:, 8 * WIDE : 9 * WIDE] = high
        out_ref[:, 9 * WIDE :] = (weights - high.astype(F32)).astype(BF16)


def update_body(info_ref, own_ref, one, two, far, fb_ref, out_ref):
    first = lane((SLOTS, WIDE)) < SIDE
    live = row((SLOTS, WIDE)) < jnp.where(first, info_ref[1], info_ref[2])
    here = info_ref[0]
    others = (one, two, far)
    total = own_ref[:, 8 * WIDE :]
    for part in others:
        total = total + (
            part[:, 8 * WIDE : 9 * WIDE].astype(F32) + part[:, 9 * WIDE :].astype(F32)
        )
    divisor = jnp.maximum(total, 1.0)
    for j in range(8):
        lanes = slice(j * WIDE, (j + 1) * WIDE)
        total = own_ref[:, lanes]
        for part in others:
            total = total + part[:, lanes].astype(F32)
        fresh = jnp.maximum(fb_ref[here, :, lanes].astype(F32) + total / divisor, 0.0)
        out_ref[:, lanes] = jnp.where(live, fresh, 0.0).astype(BF16)


def frames_body(drop_ref, out_ref):
    unit = eye(WIDE)

    def step(j, carry):
        for t in range(2):
            part = drop_ref[pl.ds(j * 4, 4), t * SIDE : (t + 1) * SIDE, :].reshape(256, WIDE)
            turned = nt(unit, part).reshape(16, 8, 256)
            out_ref[:, t, :, pl.ds(pl.multiple_of(j * 256, 256), 256)] = turned.astype(BF16)
        return carry

    lax.fori_loop(0, 16, step, 0)


def swapped(x, axis):
    return lax.all_to_all(x, axis, split_axis=0, concat_axis=0, tiled=True)


def moved(piece, down, right):
    count, across = lax.axis_size("tile"), GRID_W // 2
    pairs = []
    for source in range(count):
        y, x = source // across + down, source % across + right
        if 0 <= y < count // across and 0 <= x < across:
            pairs.append((source, y * across + x))
    return lax.ppermute(piece, "tile", pairs)


def along(piece, away):
    return lax.ppermute(piece, "tm", [(k, (k + 2 * away) % 8) for k in range(8)])


def other_core(piece):
    return lax.ppermute(piece, "tm", [(k, k ^ 1) for k in range(8)])


def body(
    movie_frames,
    baseline,
    footprints,
    traces,
    intersection,
    counts,
    offsets,
    cycle_coef,
    decay_rate,
    rise_rate,
    penalty,
):
    tiles, frames = lax.axis_size("tile"), lax.axis_size("tm")
    frames_dev = movie_frames.shape[0]
    pixels = SIDE * SIDE
    here = lax.axis_index("tile")
    block = lax.axis_index("tm").astype(jnp.int32)
    picture = (SIDE, WIDE, WIDE)
    turned_shape = (8, 8 * WIDE, WIDE)
    shape_block = (SLOTS, 8 * WIDE)

    ready = movie_frames.reshape(frames_dev, tiles, 2, pixels).transpose(1, 2, 0, 3)
    local_movie = swapped(ready, "tile")

    ready, traces_later = lax.optimization_barrier((ready, traces))
    padded = jnp.pad(traces_later, ((0, NPAD - NEUR), (0, 0))).astype(BF16)
    gathered = swapped(jnp.broadcast_to(padded, (tiles, NPAD, WIDE)), "tile")

    base = lax.dynamic_slice_in_dim(baseline, here * 2, 2, 0).reshape(2, 1, pixels)
    occupied = jnp.arange(SLOTS, dtype=jnp.int32)[None, :] < counts[:, None]
    owner = intersection // NEUR
    pick = jnp.where(occupied, owner * NPAD + (intersection - owner * NEUR), -1)
    lines = [pick.reshape(1, WIDE).astype(F32)]
    for rate in (decay_rate, rise_rate, penalty):
        lines.append(jnp.pad(rate, (0, WIDE - NEUR)).reshape(1, WIDE))
    lines = jnp.concatenate(lines + [jnp.zeros((4, WIDE), F32)])
    info = jnp.concatenate([block.reshape(1), counts, offsets.reshape(-1)])

    (base_cols,) = call(baseline_body, [(picture, F32)], (base,), name="base")
    (shapes,) = call(
        merge_body,
        [((8, SLOTS, 8 * WIDE), BF16)],
        (info, footprints.transpose(1, 0, 2)),
        smem=1,
        name="merge",
    )
    (turned,) = call(expand_body, [(turned_shape, BF16)], (shapes,), name="expand")
    (slots,) = call(collect_body, [((WIDE, WIDE), BF16)], (gathered, lines), name="collect")
    side_shapes = [((SIDE, STRIP, WIDE), BF16)] * 2
    shelf_shapes = [((RAD, WIDE + 2 * STRIP, WIDE), BF16)] * 2
    pad_shape = (SIDE + 2 * RAD, WIDE + 2 * STRIP, WIDE)
    blocks = by_frame = clean = None
    for iteration in range(ITERS):
        if iteration == 0:
            clean, resid, left, west, east = call(
                first_left_body,
                [(picture, F32), (picture, F32), (picture, BF16)] + side_shapes,
                (local_movie, base_cols, turned, slots),
                name="left0",
            )
        else:
            shapes, turned, resid, left, west, east = call(
                next_left_body,
                [((8, SLOTS, 8 * WIDE), BF16), (turned_shape, BF16), (picture, F32),
                 (picture, BF16)] + side_shapes,
                (info, *blocks, clean, slots),
                smem=1,
                name="left1",
            )
        (major,) = call(major_body, [((WIDE, WIDE), F32)], (shapes,), name="major")
        from_west, from_east = moved(east, 0, 1), moved(west, 0, -1)
        top, bottom = call(shelf_body, shelf_shapes, (left, from_west, from_east), name="shelf")
        from_top, from_bottom = moved(bottom, 1, 0), moved(top, -1, 0)
        pad, drop, mis, part = call(
            inner_body,
            [(pad_shape, F32), (picture, BF16), (picture, BF16), ((WIDE, WIDE), F32)],
            (info, cycle_coef, left, from_west, from_east, resid, shapes),
            smem=2,
            name="inner",
        )
        _, drop, _, terms = call(
            outer_body,
            [(pad_shape, F32), (picture, BF16), (picture, BF16), ((tiles, NPAD, WIDE), F32)],
            (info, cycle_coef, from_top, from_bottom, resid, shapes, major, lines, part,
             pad, drop, mis),
            smem=2,
            name="outer",
            aliases={9: 0, 10: 1, 11: 2},
        )
        arrived = swapped(terms, "tile")
        if iteration == ITERS - 1:
            (by_frame,) = call(
                frames_body, [((tiles, 2, frames_dev, pixels), BF16)], (drop,), name="turn"
            )
            by_frame, arrived = lax.optimization_barrier((by_frame, arrived))
            by_frame = swapped(by_frame, "tile")
        a, b, ends = call(
            filter_body,
            [((NEUR, WIDE), F32), ((NEUR, WIDE), F32), ((frames, 8, WIDE), F32)],
            (arrived, traces, lines),
            name="filter",
        )
        ends = swapped(ends, "tm")
        traces, copies = call(
            entering_body,
            [((NEUR, WIDE), F32), ((tiles, NPAD, WIDE), BF16)],
            (info, ends, lines, a, b),
            smem=1,
            name="entering",
        )
        gathered = swapped(copies, "tile")
        slots, keep, send = call(
            numer_body,
            [((WIDE, WIDE), BF16), ((4, SLOTS, 9 * WIDE), F32), ((4, SLOTS, 9 * WIDE), F32)],
            (info, gathered, lines, clean, drop, turned),
            smem=1,
            name="numer",
        )
        own, *outward = call(
            fold_body,
            [((SLOTS, 9 * WIDE), F32)] + [((SLOTS, 10 * WIDE), BF16)] * 3,
            (info, keep, other_core(send)),
            smem=1,
            name="fold",
        )
        inward = [along(piece, away) for piece, away in zip(outward, (1, -1, 2))]
        (fresh,) = call(
            update_body, [(shape_block, BF16)], (info, own, *inward, shapes), smem=1, name="update"
        )
        blocks = [fresh] + [along(fresh, away) for away in (1, -1, 2)]
        blocks = blocks + [other_core(piece) for piece in blocks]
    backdrop = by_frame.transpose(2, 0, 1, 3).reshape(movie_frames.shape)
    (out_shapes,) = call(
        split_body, [((2, SLOTS, pixels), BF16)], (info, *blocks), smem=1, name="split"
    )
    return (traces, out_shapes.transpose(1, 0, 2), backdrop)


def solution(mesh):
    in_specs = (
        P(("tm", "tile"), None, None),
        P(),
        P(None, "tile", None),
        P("tile", "tm"),
        P("tile", None),
        P("tile"),
        P(),
        P(),
        P("tile"),
        P("tile"),
        P("tile"),
    )
    out_specs = (P("tile", "tm"), P(None, "tile", None), P(("tm", "tile"), None, None))
    return jax.shard_map(body, mesh=mesh, in_specs=in_specs, out_specs=out_specs, check_vma=False)
```

```python
import functools

import jax
import jax.numpy as jnp
from jax import lax
from jax.experimental import pallas as pl
from jax.experimental.pallas import tpu as pltpu
from jax.sharding import PartitionSpec as P

SIDE = 64
WIDE = 128
RAD = 12
STRIP = 16
GRID_W = 8
ITERS = 2
SLOTS = 64
CYCLE = 8
NEUR = 40
NPAD = 48
EPSILON = 1e-06
F32 = jnp.float32
BF16 = jnp.bfloat16


def nt(a, b):
    return lax.dot_general(a, b, (((1,), (1,)), ((), ())), preferred_element_type=F32)


def nn(a, b):
    return lax.dot_general(a, b, (((1,), (0,)), ((), ())), preferred_element_type=F32)


def eye(n):
    return (
        lax.broadcasted_iota(jnp.int32, (n, n), 0) == lax.broadcasted_iota(jnp.int32, (n, n), 1)
    ).astype(BF16)


def three(x):
    high = x.astype(BF16)
    rest = x - high.astype(F32)
    mid = rest.astype(BF16)
    low = (rest - mid.astype(F32)).astype(BF16)
    return high, mid, low


def lane(shape):
    return lax.broadcasted_iota(jnp.int32, shape, len(shape) - 1)


def row(shape):
    return lax.broadcasted_iota(jnp.int32, shape, len(shape) - 2)


def call(body, outs, args, smem=0, scratch=(), name=None, room=6, aliases=None, away=(), space=pltpu.VMEM):
    spaces, held = [], []
    for k, arg in enumerate(args):
        if k < smem:
            spaces.append(pl.BlockSpec(memory_space=pltpu.SMEM))
        elif k in away:
            spaces.append(pl.BlockSpec(memory_space=pl.ANY))
            arg = pltpu.with_memory_space_constraint(arg, pltpu.HBM)
        else:
            spaces.append(pl.BlockSpec(memory_space=pltpu.VMEM))
            arg = pltpu.with_memory_space_constraint(arg, pltpu.VMEM)
        held.append(arg)
    return pl.pallas_call(
        body,
        out_shape=[space(s, d) for s, d in outs],
        in_specs=spaces,
        out_specs=[pl.BlockSpec(memory_space=pltpu.VMEM)] * len(outs),
        scratch_shapes=list(scratch),
        input_output_aliases=aliases or {},
        compiler_params=pltpu.CompilerParams(vmem_limit_bytes=room << 20),
        name=name,
    )(*held)


def fetches(sources, targets, sems, count):
    copies = []
    for k, (source, target) in enumerate(zip(sources, targets)):
        size = source.shape[0] // count
        copies.append(
            lambda j, k=k, source=source, target=target, size=size: pltpu.make_async_copy(
                source.at[pl.ds(j * size, size)], target.at[pl.ds(j * size, size)], sems.at[k, j]
            )
        )
    return copies


def column(line, rows):
    diagonal = row((rows, WIDE)) == lane((rows, WIDE))
    spread = jnp.where(diagonal, jnp.broadcast_to(line, (rows, WIDE)), 0.0)
    return jnp.sum(spread, axis=1, keepdims=True)


def picked(gathered, pick_ref):
    keys = gathered.shape[0]
    wanted = column(pick_ref[0:1], WIDE).astype(jnp.int32)
    chosen = (wanted == lane((WIDE, keys))).astype(F32).astype(BF16)
    return nn(chosen, gathered).astype(BF16)


def doubled(block):
    wide = block.astype(F32)
    first = (lane(wide.shape) & (WIDE - 1)) < SIDE
    upper = jnp.where(first, wide, 0.0)
    return jnp.concatenate([upper, wide - upper], axis=0).astype(BF16)


def baseline_body(base_ref, out_ref):
    unit = eye(256)

    def step(j, carry):
        for t in range(2):
            line = base_ref[t, 0:1, pl.ds(pl.multiple_of(j * 256, 256), 256)]
            parts = three(jnp.broadcast_to(line, (WIDE, 256)))
            col = nt(unit, parts[0]) + nt(unit, parts[1]) + nt(unit, parts[2])
            out_ref[pl.ds(j * 4, 4), t * SIDE : (t + 1) * SIDE, :] = col.reshape(4, SIDE, WIDE)
        return carry

    lax.fori_loop(0, 16, step, 0)


def merge_body(info_ref, fp_ref, out_ref):
    first = lane((SLOTS, WIDE)) < SIDE
    slot = row((SLOTS, WIDE))
    live = slot < jnp.where(first, info_ref[1], info_ref[2])
    for j in range(32):
        a = fp_ref[0, :, j * WIDE : (j + 1) * WIDE].astype(F32)
        b = fp_ref[1, :, j * WIDE : (j + 1) * WIDE].astype(F32)
        even = jnp.where(first, a, pltpu.roll(b, SIDE, 1))
        odd = jnp.where(first, pltpu.roll(a, SIDE, 1), b)
        at = (2 * j) % 8 * WIDE
        out_ref[j // 4, :, at : at + WIDE] = jnp.where(live, even, 0.0).astype(BF16)
        out_ref[j // 4, :, at + WIDE : at + 2 * WIDE] = jnp.where(live, odd, 0.0).astype(BF16)


def split_body(info_ref, *refs):
    blocks, out_ref = refs[:-1], refs[-1]
    first = lane((SLOTS, WIDE)) < SIDE
    for block_ref, j in zip(blocks, owners(info_ref)):
        for k in range(4):
            at = 2 * k * WIDE
            even = block_ref[:, at : at + WIDE].astype(F32)
            odd = block_ref[:, at + WIDE : at + 2 * WIDE].astype(F32)
            a = jnp.where(first, even, pltpu.roll(odd, SIDE, 1))
            b = jnp.where(first, pltpu.roll(even, SIDE, 1), odd)
            to = pl.ds(pl.multiple_of((j * 4 + k) * WIDE, WIDE), WIDE)
            out_ref[0, :, to] = a.astype(BF16)
            out_ref[1, :, to] = b.astype(BF16)


def expand_body(fb_ref, out_ref):
    unit = eye(256)

    def step(j, carry):
        both = doubled(fb_ref[j])
        for k in range(4):
            out_ref[j, k * 256 : (k + 1) * 256, :] = nt(
                unit, both[:, k * 256 : (k + 1) * 256]
            ).astype(BF16)
        return carry

    lax.fori_loop(0, 8, step, 0)


def major_body(fb_ref, out_ref):
    def step(j, total):
        for k in range(8):
            block = fb_ref[j, :, k * WIDE : (k + 1) * WIDE].astype(F32)
            total = total + block * jnp.sum(block, axis=0, keepdims=True)
        return total

    total = lax.fori_loop(0, 8, step, jnp.zeros((SLOTS, WIDE), F32))
    first = lane((SLOTS, WIDE)) < SIDE
    upper = jnp.sum(jnp.where(first, total, 0.0), axis=1, keepdims=True)
    lower = jnp.sum(jnp.where(first, 0.0, total), axis=1, keepdims=True)
    out_ref[...] = jnp.broadcast_to(jnp.concatenate([upper, lower], axis=0), (WIDE, WIDE))


def pack_body(movie_ref, traces_ref, out_ref):
    step = pl.program_id(0)

    @pl.when(step < 8)
    def _():
        for k in range(2):
            part = movie_ref[:, :, k * 256 : (k + 1) * 256].astype(F32)
            part = jnp.swapaxes(part, 0, 1).reshape(out_ref.shape[0], 2, 8, 256)
            for t in range(2):
                out_ref[:, 2 * k + t] = part[:, t].astype(BF16)

    @pl.when(step == 8)
    def _():
        padded = jnp.concatenate([traces_ref[...], jnp.zeros((NPAD - NEUR, WIDE), F32)], axis=0)
        for g in range(3):
            both = [padded[g * 16 + h * 8 : g * 16 + h * 8 + 8] for h in range(2)]
            line = jnp.concatenate(both, axis=1).astype(BF16)
            for d in range(out_ref.shape[0]):
                out_ref[d, g] = line
        for d in range(out_ref.shape[0]):
            out_ref[d, 3] = jnp.zeros((8, 256), BF16)


def pack(movie, traces, tiles):
    last = movie.shape[2] // 512
    return pl.pallas_call(
        pack_body,
        grid=(last + 1,),
        out_shape=jax.ShapeDtypeStruct((tiles, 4 * (last + 1), 8, 256), BF16),
        in_specs=[
            pl.BlockSpec((8, 2 * tiles, 512), lambda j: (0, 0, jnp.minimum(j, last - 1))),
            pl.BlockSpec((NEUR, WIDE), lambda j: (0, 0)),
        ],
        out_specs=pl.BlockSpec((tiles, 4, 8, 256), lambda j: (0, j, 0, 0)),
        compiler_params=pltpu.CompilerParams(vmem_limit_bytes=8 << 20),
        name="pack",
    )(pltpu.with_memory_space_constraint(movie, pltpu.HBM), traces)


def unpack_body(in_ref, out_ref):
    for k in range(2):
        part = in_ref[:, 2 * k : 2 * k + 2].astype(F32)
        part = jnp.swapaxes(part.reshape(-1, 8, 256), 0, 1)
        out_ref[:, :, k * 256 : (k + 1) * 256] = part.astype(BF16)


def unpack(chunks):
    tiles, count = chunks.shape[:2]
    return pl.pallas_call(
        unpack_body,
        grid=(count // 4,),
        out_shape=jax.ShapeDtypeStruct((8, 2 * tiles, 128 * count), BF16),
        in_specs=[pl.BlockSpec((tiles, 4, 8, 256), lambda j: (0, j, 0, 0))],
        out_specs=pl.BlockSpec((8, 2 * tiles, 512), lambda j: (0, 0, j)),
        compiler_params=pltpu.CompilerParams(vmem_limit_bytes=8 << 20),
        name="unpack",
    )(pltpu.with_memory_space_constraint(chunks, pltpu.HBM))


def sides(left_ref, west, east):
    west[...] = left_ref[:, :STRIP]
    east[...] = left_ref[:, WIDE - STRIP :]


def first_left_body(
    x_any, base_any, ft_ref, lines_ref, d_ref, resid_ref, left_ref, west, east,
    x_ref, base_ref, x_sem, sems,
):
    movie = pltpu.make_async_copy(x_any, x_ref, x_sem)
    movie.start()
    (base,) = fetches((base_any,), (base_ref,), sems, 4)
    for j in range(4):
        base(j).start()
    unit = eye(256)
    movie.wait()
    first = x_ref[:, 32:35].astype(F32)
    first = jnp.stack([first[..., :WIDE], first[..., WIDE:]], axis=2)
    slots = picked(first.reshape(-1, WIDE).astype(BF16), lines_ref)

    def step(j, carry):
        halves = []
        for t in range(2):
            part = x_ref[:, 2 * j + t].astype(F32).reshape(WIDE, 256).astype(BF16)
            halves.append(nt(unit, part).reshape(4, SIDE, WIDE))
        rows = pl.ds(j * 4, 4)
        clean = jnp.concatenate(halves, axis=1) - base_ref[rows]
        ft = ft_ref[j // 2, pl.ds(pl.multiple_of((j % 2) * 512, 512), 512), :]
        resid = clean - nn(ft, slots).reshape(4, WIDE, WIDE)
        d_ref[rows] = clean
        resid_ref[rows] = resid
        left_ref[rows] = resid.astype(BF16)
        return carry

    for quarter in range(4):
        base(quarter).wait()
        lax.fori_loop(quarter * 4, quarter * 4 + 4, step, 0)
    sides(left_ref, west, east)


def owners(info_ref):
    x, core = info_ref[0] // 2, info_ref[0] % 2
    found = []
    for side in (core, 1 - core):
        for away in (0, -1, 1, 2):
            found.append(lax.rem(x + away + 4, 4) * 2 + side)
    return found


def next_left_body(info_ref, *refs):
    blocks, (d_ref, s_ref, fb_ref, ft_ref, resid_ref, left_ref, west, east) = refs[:8], refs[8:]
    unit = eye(256)
    slots = s_ref[...]
    for block_ref, j in zip(blocks, owners(info_ref)):
        fb_ref[j] = block_ref[...]
        both = doubled(block_ref[...])
        for k in range(4):
            ft = nt(unit, both[:, k * 256 : (k + 1) * 256]).astype(BF16)
            ft_ref[j, k * 256 : (k + 1) * 256, :] = ft
            rows = pl.ds(j * 8 + k * 2, 2)
            resid = d_ref[rows] - nn(ft, slots).reshape(2, WIDE, WIDE)
            resid_ref[rows] = resid
            left_ref[rows] = resid.astype(BF16)
    sides(left_ref, west, east)


def shelf_body(left_ref, west, east, top, bottom):
    for at, out in ((0, top), (SIDE - RAD, bottom)):
        rows = slice(at, at + RAD)
        out[:, :STRIP] = west[rows]
        out[:, STRIP : STRIP + WIDE] = left_ref[rows]
        out[:, STRIP + WIDE :] = east[rows]


def drops(first, last, info_ref, coef_ref, pad_ref, resid_ref, drop_ref, mis_ref):
    def step(r, carry):
        total = jnp.zeros((WIDE, WIDE), F32)
        for i in range(CYCLE):
            down, right = info_ref[3 + 2 * i], info_ref[4 + 2 * i]
            total = total + coef_ref[i] * pad_ref[r + RAD + down, pl.ds(STRIP + right, WIDE), :]
        drop = total.astype(BF16)
        drop_ref[r] = drop
        mis_ref[r] = (resid_ref[r] - drop.astype(F32)).astype(BF16)
        return carry

    lax.fori_loop(first, last, step, 0)


def projected(blocks, fb_ref, mis_ref):
    total = jnp.zeros((WIDE, WIDE), F32)
    for j in blocks:
        total = total + nn(
            doubled(fb_ref[j]), mis_ref[j * 8 : (j + 1) * 8].reshape(8 * WIDE, WIDE)
        )
    return total


def inner_body(
    info_ref, coef_ref, left_ref, west, east, resid_ref, fb_ref, pad_ref, drop_ref, mis_ref, out_ref
):
    def fill(r, carry):
        pad_ref[RAD + r, STRIP : STRIP + WIDE, :] = left_ref[r].astype(F32)
        pad_ref[RAD + r, :STRIP, :] = west[r].astype(F32)
        pad_ref[RAD + r, STRIP + WIDE :, :] = east[r].astype(F32)
        return carry

    lax.fori_loop(0, SIDE, fill, 0)
    drops(RAD, SIDE - RAD, info_ref, coef_ref, pad_ref, resid_ref, drop_ref, mis_ref)
    out_ref[...] = projected(range(2, 6), fb_ref, mis_ref)


def outer_body(
    info_ref, coef_ref, top, bottom, resid_ref, fb_ref, major_ref, lines_ref, part_ref,
    pad_in, drop_in, mis_in, pad_ref, drop_ref, mis_ref, out_ref,
):
    def fill(r, carry):
        pad_ref[r] = top[r].astype(F32)
        pad_ref[RAD + SIDE + r] = bottom[r].astype(F32)
        return carry

    lax.fori_loop(0, RAD, fill, 0)
    drops(0, RAD, info_ref, coef_ref, pad_ref, resid_ref, drop_ref, mis_ref)
    drops(SIDE - RAD, SIDE, info_ref, coef_ref, pad_ref, resid_ref, drop_ref, mis_ref)
    total = part_ref[...] + projected((0, 1, 6, 7), fb_ref, mis_ref)
    keys = out_ref.shape[0] * NPAD
    chosen = (lines_ref[0:1].astype(jnp.int32) == row((keys, WIDE))).astype(F32).astype(BF16)
    both = jnp.concatenate([total, major_ref[...]], axis=1)
    high, mid, low = three(both)
    found = nn(chosen, high) + nn(chosen, mid) + nn(chosen, low)
    diagonal = row((NPAD, WIDE)) == lane((NPAD, WIDE))
    for b in range(out_ref.shape[0]):
        out_ref[b, :NEUR] = found[b * NPAD : b * NPAD + NEUR, :WIDE]
        spread = jnp.where(diagonal, found[b * NPAD : (b + 1) * NPAD, WIDE:], 0.0)
        out_ref[b, NEUR:NPAD, :] = jnp.broadcast_to(
            jnp.sum(spread, axis=0, keepdims=True), (NPAD - NEUR, WIDE)
        )


def first_order(x, rate):
    at = lane(x.shape)
    power = rate
    for k in range(7):
        x = x + power * jnp.where(at >= (1 << k), pltpu.roll(x, 1 << k, 1), 0.0)
        power = power * power
    return x


def filter_body(sum_ref, traces_ref, lines_ref, a_ref, b_ref, out_ref):
    total = jnp.sum(sum_ref[...], axis=0)
    gradient = total[:NEUR]
    diagonal = row((NEUR, WIDE)) == lane((NEUR, WIDE))
    curvature = column(total[NEUR : NEUR + 1], NEUR)
    decay, rise, cost = (column(lines_ref[k : k + 1], NEUR) for k in (1, 2, 3))
    stepped = traces_ref[...] + gradient / (curvature + EPSILON)
    rectified = jnp.maximum(stepped - cost, 0.0)
    driven = (1.0 - decay) * (1.0 - rise) * rectified
    a = first_order(driven, decay)
    b = first_order(driven, rise)
    a_ref[...] = a
    b_ref[...] = b
    ends = []
    for x in (a, b):
        at_end = jnp.broadcast_to(x[:, WIDE - 1 :], (NEUR, WIDE))
        ends.append(jnp.sum(jnp.where(diagonal, at_end, 0.0), axis=0, keepdims=True))
    ends.append(jnp.zeros((6, WIDE), F32))
    block = jnp.concatenate(ends, axis=0)
    out_ref[...] = block


def entering_body(info_ref, lines_ref, a_ref, b_ref, *refs):
    ends, (out_ref, copies_ref, ends_ref) = refs[:8], refs[8:]
    here = info_ref[0]
    for end, j in zip(ends, owners(info_ref)):
        ends_ref[j] = end[...]
    rates = lines_ref[1:3]
    for _ in range(7):
        rates = rates * rates
    held = jnp.zeros((2, WIDE), F32)
    for k in range(ends_ref.shape[0]):
        held = jnp.where(k < here, rates * held + ends_ref[k, :2], held)
    later = lane((NEUR, WIDE)) + 1

    def whole(x, rate, line):
        powers = jnp.ones((NEUR, WIDE), F32)
        squared = rate
        for k in range(8):
            powers = powers * jnp.where((later >> k) & 1 == 1, squared, 1.0)
            squared = squared * squared
        return x + powers * column(line, NEUR)

    decay, rise = (column(lines_ref[k : k + 1], NEUR) for k in (1, 2))
    a = whole(a_ref[...], decay, held[0:1])
    b = whole(b_ref[...], rise, held[1:2])
    traces = (decay * a - rise * b) / (decay - rise)
    out_ref[...] = traces
    padded = jnp.concatenate([traces, jnp.zeros((NPAD - NEUR, WIDE), F32)], axis=0).astype(BF16)
    for k in range(copies_ref.shape[0]):
        copies_ref[k] = padded


def numer_away_body(info_ref, g_ref, lines_ref, d_any, drop_any, ft_any, *refs):
    outs, (d_ref, drop_ref, ft_ref, sems) = refs[:3], refs[3:]
    copies = fetches((d_any, drop_any, ft_any), (d_ref, drop_ref, ft_ref), sems, 8)
    core = info_ref[0] % 2
    for k in range(8):
        j = 2 * (k % 4) + (1 - core if k < 4 else core)
        for copy in copies:
            copy(j).start()

    def ready(j):
        for copy in copies:
            copy(j).wait()

    numer_body(info_ref, g_ref, lines_ref, d_ref, drop_ref, ft_ref, *outs, ready=ready)


def numer_body(
    info_ref, g_ref, lines_ref, d_ref, drop_ref, ft_ref, s_ref, keep_ref, send_ref, ready=None
):
    slots = picked(g_ref[...].reshape(-1, WIDE), lines_ref)
    s_ref[...] = slots
    wide = slots.astype(F32)
    sums = jnp.concatenate(
        [
            jnp.broadcast_to(jnp.sum(wide[:SLOTS], axis=0, keepdims=True), (SLOTS, WIDE)),
            jnp.broadcast_to(jnp.sum(wide[SLOTS:], axis=0, keepdims=True), (SLOTS, WIDE)),
        ],
        axis=0,
    )
    weight = jnp.sum(wide * sums, axis=1, keepdims=True)
    first = lane((SLOTS, WIDE)) < SIDE
    weights = jnp.where(first, weight[:SLOTS], weight[SLOTS:])
    first = (lane((SLOTS, 8 * WIDE)) & (WIDE - 1)) < SIDE
    core = info_ref[0] % 2
    for out_ref, side in ((send_ref, 1 - core), (keep_ref, core)):

        def step(x, carry):
            j = 2 * x + side
            if ready is not None:
                ready(j)
            rebuilt = nn(ft_ref[j], slots)
            rows = pl.ds(j * 8, 8)
            clean = d_ref[rows] - drop_ref[rows].astype(F32)
            mis = (clean.reshape(8 * WIDE, WIDE) - rebuilt).astype(BF16)
            both = nt(slots, mis)
            out_ref[x, :, : 8 * WIDE] = jnp.where(first, both[:SLOTS], both[SLOTS:])
            out_ref[x, :, 8 * WIDE :] = weights
            return carry

        lax.fori_loop(0, 4, step, 0)


def fold_body(info_ref, keep_ref, got_ref, own_ref, *out_refs):
    x = info_ref[0] // 2
    own_ref[...] = keep_ref[x] + got_ref[x]
    for away, out_ref in zip((1, -1, 2), out_refs):
        there = lax.rem(x + away + 4, 4)
        out_ref[:, : 8 * WIDE] = (
            keep_ref[there, :, : 8 * WIDE] + got_ref[there, :, : 8 * WIDE]
        ).astype(BF16)
        weights = keep_ref[there, :, 8 * WIDE :] + got_ref[there, :, 8 * WIDE :]
        high = weights.astype(BF16)
        out_ref[:, 8 * WIDE : 9 * WIDE] = high
        out_ref[:, 9 * WIDE :] = (weights - high.astype(F32)).astype(BF16)


def update_body(info_ref, own_ref, one, two, far, fb_ref, out_ref):
    first = lane((SLOTS, WIDE)) < SIDE
    live = row((SLOTS, WIDE)) < jnp.where(first, info_ref[1], info_ref[2])
    here = info_ref[0]
    others = (one, two, far)
    total = own_ref[:, 8 * WIDE :]
    for part in others:
        total = total + (
            part[:, 8 * WIDE : 9 * WIDE].astype(F32) + part[:, 9 * WIDE :].astype(F32)
        )
    divisor = jnp.maximum(total, 1.0)
    for j in range(8):
        lanes = slice(j * WIDE, (j + 1) * WIDE)
        total = own_ref[:, lanes]
        for part in others:
            total = total + part[:, lanes].astype(F32)
        fresh = jnp.maximum(fb_ref[here, :, lanes].astype(F32) + total / divisor, 0.0)
        out_ref[:, lanes] = jnp.where(live, fresh, 0.0).astype(BF16)


def frames_body(drop_ref, out_ref):
    unit = eye(WIDE)

    def step(j, carry):
        for t in range(2):
            part = drop_ref[pl.ds(j * 4, 4), t * SIDE : (t + 1) * SIDE, :].reshape(256, WIDE)
            out_ref[:, 2 * j + t] = nt(unit, part).reshape(-1, 8, 256).astype(BF16)
        return carry

    lax.fori_loop(0, 16, step, 0)


def swapped(x, axis):
    return lax.all_to_all(x, axis, split_axis=0, concat_axis=0, tiled=True)


def moved(piece, down, right):
    count, across = lax.axis_size("tile"), GRID_W // 2
    pairs = []
    for source in range(count):
        y, x = source // across + down, source % across + right
        if 0 <= y < count // across and 0 <= x < across:
            pairs.append((source, y * across + x))
    return lax.ppermute(piece, "tile", pairs)


def along(piece, away):
    return lax.ppermute(piece, "tm", [(k, (k + 2 * away) % 8) for k in range(8)])


def other_core(piece):
    return lax.ppermute(piece, "tm", [(k, k ^ 1) for k in range(8)])


def everyone(piece):
    pieces = [piece] + [along(piece, away) for away in (1, -1, 2)]
    return pieces + [other_core(p) for p in pieces]


def body(
    movie_frames,
    baseline,
    footprints,
    traces,
    intersection,
    counts,
    offsets,
    cycle_coef,
    decay_rate,
    rise_rate,
    penalty,
):
    tiles, frames = lax.axis_size("tile"), lax.axis_size("tm")
    frames_dev = movie_frames.shape[0]
    pixels = SIDE * SIDE
    here = lax.axis_index("tile")
    block = lax.axis_index("tm").astype(jnp.int32)
    picture = (SIDE, WIDE, WIDE)
    turned_shape = (8, 8 * WIDE, WIDE)
    shape_block = (SLOTS, 8 * WIDE)

    local_movie = swapped(pack(movie_frames, traces, tiles), "tile")

    base = lax.dynamic_slice_in_dim(baseline, here * 2, 2, 0).reshape(2, 1, pixels)
    occupied = jnp.arange(SLOTS, dtype=jnp.int32)[None, :] < counts[:, None]
    owner = intersection // NEUR
    pick = jnp.where(occupied, owner * NPAD + (intersection - owner * NEUR), -1)
    lines = [pick.reshape(1, WIDE).astype(F32)]
    for rate in (decay_rate, rise_rate, penalty):
        lines.append(jnp.pad(rate, (0, WIDE - NEUR)).reshape(1, WIDE))
    lines = jnp.concatenate(lines + [jnp.zeros((4, WIDE), F32)])
    info = jnp.concatenate([block.reshape(1), counts, offsets.reshape(-1)])

    (base_cols,) = call(
        baseline_body, [(picture, F32)], (base,), name="base", space=pltpu.HBM
    )
    (shapes,) = call(
        merge_body,
        [((8, SLOTS, 8 * WIDE), BF16)],
        (info, footprints.transpose(1, 0, 2)),
        smem=1,
        name="merge",
    )
    (turned,) = call(expand_body, [(turned_shape, BF16)], (shapes,), name="expand")
    side_shapes = [((SIDE, STRIP, WIDE), BF16)] * 2
    shelf_shapes = [((RAD, WIDE + 2 * STRIP, WIDE), BF16)] * 2
    pad_shape = (SIDE + 2 * RAD, WIDE + 2 * STRIP, WIDE)
    blocks = by_frame = clean = None
    for iteration in range(ITERS):
        if iteration == 0:
            clean, resid, left, west, east = call(
                first_left_body,
                [(picture, F32), (picture, F32), (picture, BF16)] + side_shapes,
                (local_movie, base_cols, turned, lines),
                name="left0",
                room=16,
                away=(0, 1),
                scratch=[
                    pltpu.VMEM(local_movie.shape, BF16),
                    pltpu.VMEM(picture, F32),
                    pltpu.SemaphoreType.DMA,
                    pltpu.SemaphoreType.DMA((1, 4)),
                ],
            )
        else:
            shapes, turned, resid, left, west, east = call(
                next_left_body,
                [((8, SLOTS, 8 * WIDE), BF16), (turned_shape, BF16), (picture, F32),
                 (picture, BF16)] + side_shapes,
                (info, *blocks, clean, slots),
                smem=1,
                name="left1",
            )
        (major,) = call(major_body, [((WIDE, WIDE), F32)], (shapes,), name="major")
        from_west, from_east = moved(east, 0, 1), moved(west, 0, -1)
        top, bottom = call(shelf_body, shelf_shapes, (left, from_west, from_east), name="shelf")
        from_top, from_bottom = moved(bottom, 1, 0), moved(top, -1, 0)
        pad, drop, mis, part = call(
            inner_body,
            [(pad_shape, F32), (picture, BF16), (picture, BF16), ((WIDE, WIDE), F32)],
            (info, cycle_coef, left, from_west, from_east, resid, shapes),
            smem=2,
            name="inner",
        )
        _, drop, _, terms = call(
            outer_body,
            [(pad_shape, F32), (picture, BF16), (picture, BF16), ((tiles, NPAD, WIDE), F32)],
            (info, cycle_coef, from_top, from_bottom, resid, shapes, major, lines, part,
             pad, drop, mis),
            smem=2,
            name="outer",
            aliases={9: 0, 10: 1, 11: 2},
        )
        arrived = swapped(terms, "tile")
        a, b, ends = call(
            filter_body,
            [((NEUR, WIDE), F32), ((NEUR, WIDE), F32), ((8, WIDE), F32)],
            (arrived, traces, lines),
            name="filter",
        )
        if iteration == ITERS - 1:
            drop, ends = lax.optimization_barrier((drop, ends))
            (by_frame,) = call(
                frames_body,
                [((tiles, 32, frames_dev, 256), BF16)],
                (drop,),
                name="turn",
                space=pltpu.HBM,
            )
        ends = everyone(ends)
        traces, copies = call(
            entering_body,
            [((NEUR, WIDE), F32), ((tiles, NPAD, WIDE), BF16)],
            (info, lines, a, b, *ends),
            smem=1,
            name="entering",
            scratch=[pltpu.VMEM((frames, 8, WIDE), F32)],
        )
        gathered = swapped(copies, "tile")
        if iteration == ITERS - 1:
            by_frame, gathered = lax.optimization_barrier((by_frame, gathered))
            by_frame = swapped(by_frame, "tile")
        last = iteration == ITERS - 1
        slots, keep, send = call(
            numer_away_body if last else numer_body,
            [((WIDE, WIDE), BF16), ((4, SLOTS, 9 * WIDE), F32), ((4, SLOTS, 9 * WIDE), F32)],
            (info, gathered, lines, clean, drop, turned),
            smem=1,
            name="numer",
            room=16 if last else 6,
            away=(3, 4, 5) if last else (),
            scratch=[
                pltpu.VMEM(picture, F32),
                pltpu.VMEM(picture, BF16),
                pltpu.VMEM(turned_shape, BF16),
                pltpu.SemaphoreType.DMA((3, 8)),
            ] if last else [],
        )
        own, *outward = call(
            fold_body,
            [((SLOTS, 9 * WIDE), F32)] + [((SLOTS, 10 * WIDE), BF16)] * 3,
            (info, keep, other_core(send)),
            smem=1,
            name="fold",
        )
        inward = [along(piece, away) for piece, away in zip(outward, (1, -1, 2))]
        (fresh,) = call(
            update_body, [(shape_block, BF16)], (info, own, *inward, shapes), smem=1, name="update"
        )
        blocks = everyone(fresh)
    backdrop = unpack(by_frame)
    backdrop, blocks = lax.optimization_barrier((backdrop, blocks))
    (out_shapes,) = call(
        split_body, [((2, SLOTS, pixels), BF16)], (info, *blocks), smem=1, name="split"
    )
    return (traces, out_shapes.transpose(1, 0, 2), backdrop)


def solution(mesh):
    in_specs = (
        P(("tm", "tile"), None, None),
        P(),
        P(None, "tile", None),
        P("tile", "tm"),
        P("tile", None),
        P("tile"),
        P(),
        P(),
        P("tile"),
        P("tile"),
        P("tile"),
    )
    out_specs = (P("tile", "tm"), P(None, "tile", None), P(("tm", "tile"), None, None))
    return jax.shard_map(body, mesh=mesh, in_specs=in_specs, out_specs=out_specs, check_vma=False)
```
